32 devices in a mesh: row: 2 (over x), col: 16 (over z, y, core).
Axes of the slice: x: 2, y: 2, z: 4, core: 2. Of those that a mesh axis runs over, the one named last changes fastest.
Arguments:
- features: bfloat16 [8192, 256], P(('row', 'col')), may hold values from -6 to 6
- weight: bfloat16 [256, 256], replicated, may hold values from -0.375 to 0.375
- logits_grad: bfloat16 [8192, 256], P(('col', 'row')), may hold values from -6 to 6
- tile_rows: int32 [2, 16, 256], P('row', 'col'), may hold values from 0 to 3
- tile_cols: int32 [2, 16, 256], P('row', 'col'), may hold values from 0 to 31
- tile_counts: int32 [2, 16], P('row', 'col'), may hold values from 32 to 256, as said below
- tile_values: bfloat16 [2, 16, 256, 128, 128], P('row', 'col'), as said below
Outputs:
- logits: bfloat16 [8192, 256], P(('col', 'row'))
- features_grad: bfloat16 [8192, 256], P(('row', 'col'))
- weight_grad: float32 [256, 256], replicated
The draws below stay inside these ranges and needn't reach their ends.
Inputs may be any that keep to these rules, and one draw needn't show every extreme that they name: `tile_counts`: each block's live slots are its first ones; some block is full in every draw. `tile_values`: entries are non-negative; most are zero.
All inputs are finite; a program needn't handle non-finite values.
Results may differ from the reference program's by a relative error of at most 0.0051.
Values may be sent and summed in bfloat16 or wider, within the bound.
No kernel may reach another device: no remote copies, remote signals or barrier semaphores. Data moves between devices by JAX's collectives and lax.ppermute only.
A program may use at most 128 MiB of HBM per device.

```python
import math
import jax
import jax.numpy as jnp
from jax import lax

F = 256
TILE = 128
ROWS_DEV = 256
TILES_DEV = 256
NODES = 8192
BLOCK_ROWS = 512
BLOCK_COLS = 4096
ROW_TILES = 4
COL_TILES = 32
N_ROW = 2
N_COL = 16


def draw_tile_counts(key, part):
    first_key, second_key = jax.random.split(jax.random.fold_in(key, 17))
    shifts = jax.random.randint(first_key, (N_ROW * N_COL,), 0, 4)
    counts = jnp.right_shift(jnp.full((N_ROW * N_COL,), TILES_DEV, jnp.int32), shifts.astype(jnp.int32))
    fullest = jax.random.randint(second_key, (), 0, N_ROW * N_COL)
    counts = counts.at[fullest].set(TILES_DEV)
    return counts.reshape(N_ROW, N_COL).astype(jnp.int32)


def draw_tile_values(key, part):
    mask_key, value_key = jax.random.split(jax.random.fold_in(key, 29))
    shape = (N_ROW, N_COL, TILES_DEV, TILE, TILE)
    density = min(1.0, 6.0 / TILE)
    upper = 2.5 * (TILES_DEV * TILE * TILE * density / ROWS_DEV) ** (-0.5)
    present = jax.random.uniform(mask_key, shape, jnp.float32) < density
    values = jax.random.uniform(value_key, shape, jnp.float32, 0.0, upper)
    return jnp.where(present, values, jnp.float32(0.0)).astype(jnp.bfloat16)


def place_ends(array, rng, smallest, high):
    index_at = [jax.random.randint(jax.random.fold_in(rng, axis), (), 0, length) for axis, length in enumerate(array.shape)]
    widest = array.shape.index(max(array.shape))
    next_to = index_at[:widest] + [(index_at[widest] + 1) % array.shape[widest]] + index_at[widest + 1:]
    return array.at[tuple(index_at)].set(smallest).at[tuple(next_to)].set(high)


def steps_of(stream_key, dims, shards, smallest, top_value):
    def one(position, parts):
        heights = jax.random.uniform(jax.random.fold_in(jax.random.fold_in(stream_key, 6), position), (parts,), jnp.float32, smallest / len(shards), top_value / len(shards))
        return jnp.repeat(jnp.exp(heights), dims[position] // parts).reshape((-1,) + (1,) * (len(dims) - position - 1))

    gain = one(*shards[0])
    for cut in shards[1:]:
        gain = gain * one(*cut)
    return gain


def normal_values(own_key, extent, scale, reach, shards=(), kind=jnp.bfloat16):
    values = jax.random.normal(own_key, extent, jnp.float32) * scale
    if len(shards) > 0:
        values = steps_of(own_key, extent, shards, -0.22, 0.18) * values
    return jnp.clip(values, min=-reach, max=reach).astype(kind)


def setup_inputs(seed: int = 0) -> dict:
    key_of = jax.random.split(jax.random.key(seed), 8)
    features = normal_values(key_of[0], (NODES, F), 1.0, 6.0, ((0, 32),))
    weight = normal_values(key_of[1], (F, F), F ** -0.5, 0.375)
    logits_grad = normal_values(key_of[2], (NODES, F), 1.0, 6.0, ((0, 32),))
    tile_rows = place_ends(jax.random.randint(key_of[3], (N_ROW, N_COL, TILES_DEV), 0, ROW_TILES), jax.random.fold_in(key_of[3], 1), 0, ROW_TILES - 1).astype(jnp.int32)
    tile_cols = place_ends(jax.random.randint(key_of[4], (N_ROW, N_COL, TILES_DEV), 0, COL_TILES), jax.random.fold_in(key_of[4], 1), 0, COL_TILES - 1).astype(jnp.int32)
    tile_counts = draw_tile_counts(jax.random.fold_in(key_of[7], 71), 0)
    tile_values = draw_tile_values(jax.random.fold_in(key_of[7], 71), 0)
    return dict(features=features, weight=weight, logits_grad=logits_grad, tile_rows=tile_rows, tile_cols=tile_cols, tile_counts=tile_counts, tile_values=tile_values)


def slot_sum(slot_values, source, source_index, target_index, live_count, target_tiles, transposed):
    tile_size = slot_values.shape[1]
    feature_width = source.shape[1]
    blocked = source.reshape(source.shape[0] // tile_size, tile_size, feature_width).astype(jnp.float32)
    picked = jnp.take(blocked, source_index, axis=0)
    values_wide = slot_values.astype(jnp.float32)
    if transposed:
        products = jnp.einsum('sba,sbf->saf', values_wide, picked, precision=lax.Precision.HIGHEST)
    else:
        products = jnp.einsum('sab,sbf->saf', values_wide, picked, precision=lax.Precision.HIGHEST)
    alive = jnp.arange(slot_values.shape[0], dtype=jnp.int32) < live_count
    products = jnp.where(alive[:, None, None], products, jnp.float32(0.0))
    summed = jnp.zeros((target_tiles, tile_size, feature_width), jnp.float32).at[target_index].add(products)
    return summed.reshape(target_tiles * tile_size, feature_width)

def reference(features, weight, logits_grad, tile_rows, tile_cols, tile_counts, tile_values):
    device_ids = jnp.arange(N_ROW * N_COL, dtype=jnp.int32)

    def forward_device(accum, device):
        row_id = device // N_COL
        col_id = device % N_COL
        source = lax.dynamic_slice_in_dim(features, (row_id * BLOCK_COLS).astype(jnp.int32), BLOCK_COLS, 0)
        partial_value = slot_sum(tile_values[row_id, col_id], source, tile_cols[row_id, col_id], tile_rows[row_id, col_id], tile_counts[row_id, col_id], ROW_TILES, False)
        start = (col_id * BLOCK_ROWS).astype(jnp.int32)
        current = lax.dynamic_slice_in_dim(accum, start, BLOCK_ROWS, 0)
        return (lax.dynamic_update_slice_in_dim(accum, current + partial_value, start, 0), None)
    accum, _ = lax.scan(forward_device, jnp.zeros((NODES, F), jnp.float32), device_ids)
    aggregated = accum.astype(jnp.bfloat16)
    logits = jnp.dot(aggregated, weight, preferred_element_type=jnp.float32).astype(jnp.bfloat16)
    grad_hidden = lax.dot_general(logits_grad, weight, (((1,), (1,)), ((), ())), preferred_element_type=jnp.float32).astype(jnp.bfloat16)

    def backward_device(accum, device):
        row_id = device // N_COL
        col_id = device % N_COL
        source = lax.dynamic_slice_in_dim(grad_hidden, (col_id * BLOCK_ROWS).astype(jnp.int32), BLOCK_ROWS, 0)
        partial_value = slot_sum(tile_values[row_id, col_id], source, tile_rows[row_id, col_id], tile_cols[row_id, col_id], tile_counts[row_id, col_id], COL_TILES, True)
        start = (row_id * BLOCK_COLS).astype(jnp.int32)
        current = lax.dynamic_slice_in_dim(accum, start, BLOCK_COLS, 0)
        return (lax.dynamic_update_slice_in_dim(accum, current + partial_value, start, 0), None)
    back_accum, _ = lax.scan(backward_device, jnp.zeros((NODES, F), jnp.float32), device_ids)
    features_grad = back_accum.astype(jnp.bfloat16)
    weight_grad = lax.dot_general(aggregated, logits_grad, (((0,), (0,)), ((), ())), preferred_element_type=jnp.float32) / math.sqrt(NODES)
    return (logits, features_grad, weight_grad)
```

```python
import functools
import math

import jax
import jax.numpy as jnp
from jax import lax
from jax.experimental import pallas as pl
from jax.experimental.pallas import tpu as pltpu
from jax.sharding import PartitionSpec as P


F32 = jnp.float32
BF16 = jnp.bfloat16
SLOTS_STEP = 32
ACC_BYTES = 16 << 20


def split_col(n_col):
    nk = 2 if n_col % 2 == 0 else 1
    rest = n_col // nk
    nz = 4 if rest % 4 == 0 else rest
    return nz, rest // nz, nk


def cost(flops, nbytes):
    return pl.CostEstimate(flops=int(flops), bytes_accessed=int(nbytes), transcendentals=0)


def dense_kernel(rows_s, cols_s, count_s, values, out, acc, *, row_tiles, col_tiles, place, width):
    chunk, step = pl.program_id(0), pl.program_id(1)
    block, tile = values.shape[0], values.shape[1]
    live = count_s[0]

    @pl.when(step == 0)
    def _():
        acc[...] = jnp.zeros_like(acc)

    first = step * block

    def add(slot, carry):
        row = rows_s[first + slot] - chunk * row_tiles

        @pl.when((row >= 0) & (row < row_tiles))
        def _():
            at = row * col_tiles + cols_s[first + slot]
            acc[at] += values[slot].astype(F32)

        return carry

    lax.fori_loop(0, jnp.clip(live - first, 0, block), add, 0)

    @pl.when(step == pl.num_programs(1) - 1)
    def _():
        per = width // tile
        for row in range(row_tiles):
            for col in range(col_tiles):
                where = place[col // per]
                lane = (col % per) * tile
                out[where, pl.ds(row * tile, tile), pl.ds(lane, tile)] = acc[
                    row * col_tiles + col
                ].astype(BF16)


def dense_block(values, rows, cols, count, row_count, col_count, place, width):
    slots, tile = values.shape[0], values.shape[1]
    col_tiles, all_rows = col_count // tile, row_count // tile
    row_tiles = max(1, min(all_rows, ACC_BYTES // (col_tiles * tile * tile * 4)))
    while all_rows % row_tiles:
        row_tiles -= 1
    chunks = len(place)
    block = min(SLOTS_STEP, slots)

    def values_map(chunk, step, rows_s, cols_s, count_s):
        return (jnp.minimum(step, jnp.maximum(count_s[0] - 1, 0) // block), 0, 0)

    return pl.pallas_call(
        functools.partial(
            dense_kernel, row_tiles=row_tiles, col_tiles=col_tiles, place=place, width=width
        ),
        out_shape=jax.ShapeDtypeStruct((chunks, row_count, width), BF16),
        grid_spec=pltpu.PrefetchScalarGridSpec(
            num_scalar_prefetch=3,
            grid=(all_rows // row_tiles, slots // block),
            in_specs=[pl.BlockSpec((block, tile, tile), values_map)],
            out_specs=pl.BlockSpec(
                (chunks, row_tiles * tile, width), lambda chunk, step, *_: (0, chunk, 0)
            ),
            scratch_shapes=[pltpu.VMEM((row_tiles * col_tiles, tile, tile), F32)],
        ),
        cost_estimate=cost(slots * tile * tile, values.size * 2 + row_count * col_count * 2),
        name="dense_block",
    )(rows, cols, count, values)


def back_kernel(here, dense, *refs, n_row, nz, ny, nk):
    grads, (keep, send), turned = refs[:n_row], refs[n_row : n_row + 2], refs[n_row + 2]
    r, z, y = here[0], here[1], here[2]
    step = pl.program_id(0)
    count = grads[0].shape[0]

    @pl.when(step == 0)
    def _():
        for dr in range(n_row):
            turned[lax.rem(r - dr + n_row, n_row)] = grads[dr][...].astype(F32).T.astype(BF16)

    sending = step < (nk - 1) * ny
    for zz in range(nz):
        total = jnp.dot(turned[0], dense[zz, pl.ds(0, count), :], preferred_element_type=F32)
        for row in range(1, n_row):
            total += jnp.dot(
                turned[row], dense[zz, pl.ds(row * count, count), :], preferred_element_type=F32
            )
        dz = lax.rem(zz - z + nz, nz)

        @pl.when(sending)
        def _():
            send[0, 0, dz] = total.astype(BF16)

        @pl.when(jnp.logical_not(sending))
        def _():
            keep[0, dz] = total


def back_products(here, dense, grads, nz, ny, nk):
    chunks, row_count, width = dense.shape
    n_row = len(grads)
    feature = grads[0].shape[1]
    sends = (nk - 1) * ny

    def dense_map(step, here):
        dk = jnp.where(step < sends, step // ny + 1, 0)
        dy = lax.rem(step, ny)
        kk = lax.rem(here[3] + dk, nk)
        yy = lax.rem(here[2] + dy, ny)
        return (kk * ny + yy, 0, 0)

    def keep_map(step, here):
        return (jnp.where(step < sends, 0, step - sends), 0, 0, 0)

    def send_map(step, here):
        at = jnp.minimum(step, sends - 1)
        return (at // ny, lax.rem(at, ny), 0, 0, 0)

    return pl.pallas_call(
        functools.partial(back_kernel, n_row=n_row, nz=nz, ny=ny, nk=nk),
        out_shape=(
            jax.ShapeDtypeStruct((ny, nz, feature, width), F32),
            jax.ShapeDtypeStruct((max(nk - 1, 1), ny, nz, feature, width), BF16),
        ),
        grid_spec=pltpu.PrefetchScalarGridSpec(
            num_scalar_prefetch=1,
            grid=(nk * ny,),
            in_specs=[pl.BlockSpec((nz, row_count, width), dense_map)]
            + [pl.BlockSpec(g.shape, lambda step, here: (0, 0)) for g in grads],
            out_specs=[
                pl.BlockSpec((1, nz, feature, width), keep_map),
                pl.BlockSpec((1, 1, nz, feature, width), send_map),
            ],
            scratch_shapes=[pltpu.VMEM((n_row, feature, grads[0].shape[0]), BF16)],
        ),
        cost_estimate=cost(2 * dense.size * feature, dense.size * 2 + chunks * feature * width * 3),
        name="back_products",
    )(here, dense, *grads)


def first_kernel(here, dense, *refs, nz, ny):
    sources, (partial, pack) = refs[: nz * ny], refs[nz * ny :]
    z, y = here[1], here[2]
    total = None
    for dy in range(ny):
        for dz in range(nz):
            source = sources[dy * nz + dz][...]
            pack[dy * nz + dz] = source
            at = lax.rem(y - dy + ny, ny) * nz + lax.rem(z - dz + nz, nz)
            term = jnp.dot(dense[at], source, preferred_element_type=F32)
            total = term if total is None else total + term
    partial[...] = total


def first_products(here, dense, sources, nz, ny):
    chunks, row_count, width = dense.shape
    feature = sources[0].shape[1]
    group = nz * ny
    return pl.pallas_call(
        functools.partial(first_kernel, nz=nz, ny=ny),
        out_shape=(
            jax.ShapeDtypeStruct((row_count, feature), F32),
            jax.ShapeDtypeStruct((group,) + sources[0].shape, BF16),
        ),
        grid_spec=pltpu.PrefetchScalarGridSpec(
            num_scalar_prefetch=1,
            grid=(1,),
            in_specs=[pl.BlockSpec((group, row_count, width), lambda i, here: (here[3], 0, 0))]
            + [pl.BlockSpec(s.shape, lambda i, here: (0, 0)) for s in sources],
            out_specs=[
                pl.BlockSpec((row_count, feature), lambda i, here: (0, 0)),
                pl.BlockSpec((group,) + sources[0].shape, lambda i, here: (0, 0, 0)),
            ],
        ),
        cost_estimate=cost(2 * group * row_count * width * feature, group * row_count * width * 2),
        name="first_products",
    )(here, dense, *sources)


def last_kernel(here, partial, *refs, n_row, nz, ny, nk):
    others = nk - 1
    denses, packs = refs[:others], refs[others : 2 * others]
    grads = refs[2 * others : 2 * others + n_row]
    row_keep, row_send, grad_keep, grad_send = refs[2 * others + n_row :]
    r, z, y, k = here[0], here[1], here[2], here[3]
    total = partial[...]
    for dense, pack in zip(denses, packs):
        for dy in range(ny):
            for dz in range(nz):
                at = lax.rem(y - dy + ny, ny) * nz + lax.rem(z - dz + nz, nz)
                total += jnp.dot(dense[at], pack[dy * nz + dz], preferred_element_type=F32)
    count = grads[0].shape[0]
    for row in range(n_row):
        piece = total[row * count : (row + 1) * count]
        dr = lax.rem(row - r + n_row, n_row)

        @pl.when(dr == 0)
        def _():
            row_keep[...] = piece

        if n_row > 1:

            @pl.when(dr > 0)
            def _():
                row_send[jnp.maximum(dr - 1, 0)] = piece.astype(BF16)

    turned = total.T.astype(BF16)
    both = jnp.concatenate([g[...] for g in grads], axis=0) if n_row == 1 else None
    wide = jnp.zeros((total.shape[1], grads[0].shape[1]), F32)
    for row in range(n_row):
        grad = None
        for dr in range(n_row):
            here_now = lax.rem(r - dr + n_row, n_row) == row
            grad = grads[dr][...] if grad is None else jnp.where(here_now, grads[dr][...], grad)
        wide += jnp.dot(
            turned[:, row * count : (row + 1) * count], grad, preferred_element_type=F32
        )
    half = wide.shape[0] // nk
    for kk in range(nk):
        piece = wide[kk * half : (kk + 1) * half]

        @pl.when(kk == k)
        def _():
            grad_keep[...] = piece

        if nk > 1:

            @pl.when(kk != k)
            def _():
                grad_send[...] = piece.astype(BF16)


def last_products(here, dense, partial, packs, grads, nz, ny, nk):
    chunks, row_count, width = dense.shape
    feature = partial.shape[1]
    n_row = len(grads)
    group = nz * ny
    count = grads[0].shape[0]

    def dense_map(dk, i, here):
        return (lax.rem(here[3] - dk + nk, nk), 0, 0)

    flat = lambda i, here: (0, 0)
    return pl.pallas_call(
        functools.partial(last_kernel, n_row=n_row, nz=nz, ny=ny, nk=nk),
        out_shape=(
            jax.ShapeDtypeStruct((count, feature), F32),
            jax.ShapeDtypeStruct((max(n_row - 1, 1), count, feature), BF16),
            jax.ShapeDtypeStruct((feature // nk, grads[0].shape[1]), F32),
            jax.ShapeDtypeStruct((feature // nk, grads[0].shape[1]), BF16),
        ),
        grid_spec=pltpu.PrefetchScalarGridSpec(
            num_scalar_prefetch=1,
            grid=(1,),
            in_specs=[pl.BlockSpec((row_count, feature), flat)]
            + [
                pl.BlockSpec((group, row_count, width), functools.partial(dense_map, dk))
                for dk in range(1, nk)
            ]
            + [pl.BlockSpec(p.shape, lambda i, here: (0, 0, 0)) for p in packs]
            + [pl.BlockSpec(g.shape, flat) for g in grads],
            out_specs=[
                pl.BlockSpec((count, feature), flat),
                pl.BlockSpec((max(n_row - 1, 1), count, feature), lambda i, here: (0, 0, 0)),
                pl.BlockSpec((feature // nk, grads[0].shape[1]), flat),
                pl.BlockSpec((feature // nk, grads[0].shape[1]), flat),
            ],
        ),
        cost_estimate=cost(2 * group * row_count * width * feature, group * row_count * width * 2),
        name="last_products",
    )(here, partial, *([dense] * (nk - 1)), *packs, *grads)


def even_sum(terms):
    while len(terms) > 1:
        half = len(terms) // 2
        if len(terms) % 2:
            return functools.reduce(jnp.add, terms)
        terms = [terms[i] + terms[i + half] for i in range(half)]
    return terms[0]


def local(features, weight, logits_grad, tile_rows, tile_cols, tile_counts, tile_values):
    n_row, n_col = lax.axis_size("row"), lax.axis_size("col")
    nz, ny, nk = split_col(n_col)
    node_rows, feature = features.shape
    r, c = lax.axis_index("row"), lax.axis_index("col")
    z, y, k = c // (ny * nk), (c // nk) % ny, c % nk
    here = jnp.stack([r, z, y, k]).astype(jnp.int32)

    def shift(array, dz=0, dy=0, dk=0):
        pairs = []
        for zz in range(nz):
            for yy in range(ny):
                for kk in range(nk):
                    to = ((zz + dz) % nz * ny + (yy + dy) % ny) * nk + (kk + dk) % nk
                    pairs.append(((zz * ny + yy) * nk + kk, to))
        return lax.ppermute(array, "col", pairs)

    def shift_row(array, dr):
        return lax.ppermute(array, "row", [(i, (i + dr) % n_row) for i in range(n_row)])

    grads = [logits_grad] + [shift_row(logits_grad, dr) for dr in range(1, n_row)]
    column = [features] + [shift(features, dz=dz) for dz in range(1, nz)]
    sources = list(column)
    for dy in range(1, ny):
        sources += [shift(block, dy=dy) for block in column]

    place = [0] * n_col
    for zz in range(nz):
        for yy in range(ny):
            for kk in range(nk):
                place[(zz * ny + yy) * nk + kk] = (kk * ny + yy) * nz + zz
    dense = dense_block(
        tile_values[0, 0],
        tile_rows[0, 0],
        tile_cols[0, 0],
        tile_counts[0],
        node_rows * n_row,
        node_rows * n_col,
        tuple(place),
        node_rows,
    )

    keep, send = back_products(here, dense, grads, nz, ny, nk)
    for dk in range(1, nk):
        keep = keep + shift(send[dk - 1], dk=dk).astype(F32)
    inner = keep[0]
    for dy in range(1, ny):
        inner = inner + shift(keep[dy].astype(BF16), dy=dy).astype(F32)
    outer = inner[0]
    for dz in range(1, nz):
        outer = outer + shift(inner[dz].astype(BF16), dz=dz).astype(F32)
    features_grad = lax.dot_general(
        outer.astype(BF16), weight, (((0,), (1,)), ((), ())), preferred_element_type=F32
    ).astype(BF16)

    partial, pack = first_products(here, dense, sources, nz, ny)
    packs = [shift(pack, dk=dk) for dk in range(1, nk)]
    row_keep, row_send, grad_keep, grad_send = last_products(
        here, dense, partial, packs, grads, nz, ny, nk
    )
    aggregated = row_keep
    for dr in range(1, n_row):
        aggregated = aggregated + shift_row(row_send[dr - 1], dr).astype(F32)
    logits = jnp.dot(aggregated.astype(BF16), weight, preferred_element_type=F32).astype(BF16)

    if nk > 1:
        grad_keep = grad_keep + shift(grad_send, dk=1).astype(F32)
    for size, move in (
        (n_row, shift_row),
        (ny, lambda a, d: shift(a, dy=d)),
        (nz, lambda a, d: shift(a, dz=d)),
    ):
        if size > 1:
            sent = grad_keep.astype(BF16)
            terms = [sent] + [move(sent, d) for d in range(1, size)]
            grad_keep = even_sum([t.astype(F32) for t in terms])
    grad_keep = grad_keep / math.sqrt(node_rows * n_row * n_col)
    if nk > 1:
        other = shift(grad_keep, dk=1)
        low = jnp.where(k == 0, grad_keep, other)
        high = jnp.where(k == 0, other, grad_keep)
        weight_grad = jnp.concatenate([low, high], axis=0)
    else:
        weight_grad = grad_keep
    return (logits, features_grad, weight_grad)


def solution(mesh):
    placed = (
        P(("row", "col"), None),
        P(),
        P(("col", "row"), None),
        P("row", "col", None),
        P("row", "col", None),
        P("row", "col"),
        P("row", "col", None, None, None),
    )
    return jax.shard_map(
        local,
        mesh=mesh,
        in_specs=placed,
        out_specs=(P(("col", "row"), None), P(("row", "col"), None), P()),
        check_vma=False,
    )
```
